32 devices in a mesh: dp: 4 (over x, core), ctx: 8 (over z, y).
Axes of the slice: x: 2, y: 2, z: 4, core: 2. Of those that a mesh axis runs over, the one named last changes fastest.
Arguments:
- hidden_in: bfloat16 [8, 1024, 768], P('dp', 'ctx'), may hold values from -6 to 6
- input_proj: bfloat16 [3, 768, 768], P(None, ('dp', 'ctx')), may hold values from -0.3125 to 0.3125
- output_proj: bfloat16 [768, 768], P(('dp', 'ctx')), may hold values from -0.875 to 0.875
- up_proj: bfloat16 [768, 3072], P(('dp', 'ctx')), may hold values from -0.21875 to 0.21875
- down_proj: bfloat16 [3072, 768], P(('dp', 'ctx')), may hold values from -0.109375 to 0.109375
- bias_rows: bfloat16 [4, 768], P(None, ('dp', 'ctx')), may hold values from -1.75 to 1.75
- up_bias: bfloat16 [3072], P(('dp', 'ctx')), may hold values from -1.75 to 1.75
- norm_gains: bfloat16 [2, 768], P(None, ('dp', 'ctx')), may hold values from 0.5 to 1.5
- norm_shifts: bfloat16 [2, 768], P(None, ('dp', 'ctx')), may hold values from -1.75 to 1.75
- cotangent: bfloat16 [8, 1024, 768], P('dp', 'ctx'), may hold values from -6 to 6
- lengths: int32 [8], P('dp'), may hold values from 256 to 1024, as said below
Outputs:
- layer_out: bfloat16 [8, 1024, 768], P('dp', 'ctx')
- grad_input: float32 [8, 1024, 768], P('dp', 'ctx')
- grad_input_proj: float32 [3, 768, 768], P(None, ('dp', 'ctx'))
- grad_output_proj: float32 [768, 768], P(('dp', 'ctx'))
- grad_up_proj: float32 [768, 3072], P(('dp', 'ctx'))
- grad_down_proj: float32 [3072, 768], P(('dp', 'ctx'))
- grad_bias_rows: float32 [4, 768], P(None, ('dp', 'ctx'))
- grad_up_bias: float32 [3072], P(('dp', 'ctx'))
- grad_gains: float32 [2, 768], P(None, ('dp', 'ctx'))
- grad_shifts: float32 [2, 768], P(None, ('dp', 'ctx'))
The draws below stay inside these ranges and needn't reach their ends.
Inputs may be any that keep to these rules, and one draw needn't show every extreme that they name: `lengths`: each sequence's valid tokens are the prefix of that length; in every draw some sequence is full and some has exactly 256 valid tokens.
All inputs are finite; a program needn't handle non-finite values.
Results may differ from the reference program's by a relative error of at most 0.035.
Values may be sent and summed in bfloat16 or wider, within the bound.
A program may use at most 256 MiB of HBM per device.

```python
import jax
import jax.numpy as jnp
from jax import lax

D = 768
HEADS = 12
FF = 3072
SEQ = 1024
NSEQ = 8


def draw_lengths(key, part):
    base_key = jax.random.fold_in(key, 71)
    draw_key, pick_key = jax.random.split(base_key)
    drawn_len = jax.random.randint(draw_key, (NSEQ,), SEQ // 4, SEQ + 1, dtype=jnp.int32)
    shuffled = jax.random.permutation(pick_key, NSEQ)
    drawn_len = drawn_len.at[shuffled[0]].set(SEQ)
    drawn_len = drawn_len.at[shuffled[1]].set(SEQ // 4)
    return drawn_len.astype(jnp.int32)


def shard_levels(stream_key, shape, pieces, least, high):
    gain, own = 1.0, jax.random.fold_in(stream_key, 6)
    for axis_at, shards_of in pieces:
        steps = jnp.exp(jax.random.uniform(jax.random.fold_in(own, axis_at), (shards_of,), jnp.float32, least / len(pieces), high / len(pieces)))
        gain = gain * jnp.repeat(steps, shape[axis_at] // shards_of).reshape([-1 if axis == axis_at else 1 for axis in range(len(shape))])
    return gain


def scatter_about(key, dims, scale, reach, pieces=(), held_as=jnp.bfloat16):
    result = jax.random.normal(key, dims, jnp.float32) * scale
    if len(pieces) > 0:
        result = shard_levels(key, dims, pieces, -0.22, 0.18) * result
    return jnp.clip(result, min=-reach, max=reach).astype(held_as)


def setup_inputs(seed: int = 0) -> dict:
    key_list = jax.random.split(jax.random.key(seed), 12)
    hidden_in = scatter_about(key_list[0], (NSEQ, SEQ, D), 1.0, 6.0, ((0, 4), (1, 8)))
    input_proj = scatter_about(key_list[1], (3, D, D), (D // 2) ** -0.5, 0.3125, ((1, 32),))
    output_proj = scatter_about(key_list[2], (D, D), (D // 16) ** -0.5, 0.875, ((0, 32),))
    up_proj = scatter_about(key_list[3], (D, FF), D ** -0.5, 0.21875, ((0, 32),))
    down_proj = scatter_about(key_list[4], (FF, D), FF ** -0.5, 0.109375, ((0, 32),))
    bias_rows = scatter_about(key_list[5], (4, D), 0.3, 1.75, ((1, 32),))
    up_bias = scatter_about(key_list[6], (FF,), 0.3, 1.75, ((0, 32),))
    norm_gains = jnp.clip(1.0 + 0.1 * jax.random.normal(key_list[7], (2, D), jnp.float32), 0.5, 1.5).astype(jnp.bfloat16)
    norm_shifts = scatter_about(key_list[8], (2, D), 0.3, 1.75, ((1, 32),))
    cotangent = scatter_about(key_list[9], (NSEQ, SEQ, D), 1.0, 6.0, ((0, 4), (1, 8)))
    lengths = draw_lengths(jax.random.fold_in(key_list[11], 71), 0)
    return dict(hidden_in=hidden_in, input_proj=input_proj, output_proj=output_proj, up_proj=up_proj, down_proj=down_proj, bias_rows=bias_rows, up_bias=up_bias, norm_gains=norm_gains, norm_shifts=norm_shifts, cotangent=cotangent, lengths=lengths)


@jax.custom_vjp
def low(v):
    return lax.optimization_barrier(v.astype(jnp.bfloat16)).astype(jnp.float32)

@jax.custom_vjp
def low_back(v):
    return v

def low_keep(v):
    return (low(v), None)

def low_pass(kept, grad):
    return (grad,)

def back_keep(v):
    return (v, None)

def back_low(kept, grad):
    return (low(grad),)
low.defvjp(low_keep, low_pass)
low_back.defvjp(back_keep, back_low)
ln_eps = 1e-12
neg_big = -1e+30
highest = lax.Precision.HIGHEST

def matmul(left_arr, right_arr):
    return jnp.dot(left_arr, right_arr, precision=highest, preferred_element_type=jnp.float32)

def both_ways(value_arr):
    return low(low_back(value_arr))

def layer_norm(hidden, gain_vec, shift_vec):
    row_mean = lax.optimization_barrier(jnp.mean(hidden, axis=-1, keepdims=True))
    centered = hidden - row_mean
    row_var = lax.optimization_barrier(jnp.mean(centered * centered, axis=-1, keepdims=True))
    return centered * lax.rsqrt(row_var + ln_eps) * gain_vec + shift_vec

def attend_block(query_block, keys_heads, values_heads, key_live):
    scores = low_back(jnp.einsum('hqd,hkd->hqk', query_block, keys_heads, precision=highest) * 0.125)
    scores = jnp.where(key_live[None, None, :], scores, neg_big)
    probs = jnp.exp(scores - jax.nn.logsumexp(scores, axis=-1, keepdims=True))
    return jnp.einsum('hqk,hkd->hqd', low(probs), values_heads, precision=highest)
checkpointed = jax.checkpoint(attend_block)

def encoder_layer(params, hidden_in, length):
    input_proj, output_proj, up_proj, down_proj, bias_rows, up_bias, norm_gains, norm_shifts = params
    seq_len, model_width = hidden_in.shape
    head_dim = model_width // HEADS
    queries = both_ways(matmul(hidden_in, input_proj[0]) + bias_rows[0])
    keys_all = both_ways(matmul(hidden_in, input_proj[1]))
    values_all = both_ways(matmul(hidden_in, input_proj[2]) + bias_rows[1])
    key_live = jnp.arange(seq_len, dtype=jnp.int32) < length
    block_len = min(512, seq_len)
    num_blocks = seq_len // block_len
    query_heads = queries.reshape(num_blocks, block_len, HEADS, head_dim).transpose(0, 2, 1, 3)
    keys_heads = keys_all.reshape(seq_len, HEADS, head_dim).transpose(1, 0, 2)
    values_heads = values_all.reshape(seq_len, HEADS, head_dim).transpose(1, 0, 2)
    attended = lax.map(lambda query_block: checkpointed(query_block, keys_heads, values_heads, key_live), query_heads)
    heads_out = both_ways(attended.transpose(0, 2, 1, 3).reshape(seq_len, model_width))
    attn_branch = low_back(matmul(heads_out, output_proj) + bias_rows[2])
    normed = layer_norm(hidden_in + attn_branch, norm_gains[0], norm_shifts[0])
    upper = low_back(matmul(low(normed), up_proj) + up_bias)
    activated = low(jax.nn.gelu(upper, approximate=False))
    ffn_branch = low_back(matmul(activated, down_proj) + bias_rows[3])
    return layer_norm(normed + ffn_branch, norm_gains[1], norm_shifts[1])

def reference(hidden_in, input_proj, output_proj, up_proj, down_proj, bias_rows, up_bias, norm_gains, norm_shifts, cotangent, lengths):
    params = tuple((argument.astype(jnp.float32) for argument in (input_proj, output_proj, up_proj, down_proj, bias_rows, up_bias, norm_gains, norm_shifts)))
    seq_len = hidden_in.shape[1]
    positions = jnp.arange(seq_len, dtype=jnp.int32)

    def one_sequence(summed, scan_item):
        seq_in, seq_cot, length = scan_item
        layer_out, pullback = jax.vjp(lambda weights, inputs: encoder_layer(weights, inputs, length), params, seq_in.astype(jnp.float32))
        row_live = (positions < length).astype(jnp.float32)[:, None]
        grad_params, grad_input = pullback(seq_cot.astype(jnp.float32) * row_live)
        summed = jax.tree.map(lambda earlier, addend: earlier + addend, summed, grad_params)
        return (summed, (layer_out.astype(jnp.bfloat16), grad_input))
    zero_grads = jax.tree.map(jnp.zeros_like, params)
    grads, (layer_out, grad_input) = lax.scan(one_sequence, zero_grads, (hidden_in, cotangent, lengths))
    return (layer_out, grad_input, grads[0], grads[1], grads[2], grads[3], grads[4], grads[5], grads[6], grads[7])
```

```python
import functools
import itertools
import math
from typing import NamedTuple

import jax
import jax.numpy as jnp
from jax import lax
from jax.experimental import pallas as pl
from jax.experimental.pallas import tpu as pltpu
from jax.sharding import PartitionSpec as P

HEADS = 12


ln_eps = 1e-12
neg_big = -1e30


def layer_norm(hidden, gain_vec, shift_vec):
    row_mean = jnp.mean(hidden, axis=-1, keepdims=True)
    centered = hidden - row_mean
    row_var = jnp.mean(centered * centered, axis=-1, keepdims=True)
    return centered * lax.rsqrt(row_var + ln_eps) * gain_vec + shift_vec


def gelu_exact(upper):
    return jax.nn.gelu(upper, approximate=False)


def matmul(left_arr, right_arr):
    return jnp.dot(left_arr, right_arr, preferred_element_type=jnp.float32)


def matmul_nt(left_arr, right_arr):
    return lax.dot_general(
        left_arr, right_arr, (((1,), (1,)), ((), ())), preferred_element_type=jnp.float32
    )


def matmul_tn(left_arr, right_arr):
    return lax.dot_general(
        left_arr, right_arr, (((0,), (0,)), ((), ())), preferred_element_type=jnp.float32
    )


def column_sum(values_arr):
    return jnp.sum(values_arr.astype(jnp.float32), axis=0)


def block_scores(queries, key_block, block_start, length):
    scores = (
        jnp.einsum("rhd,khd->hrk", queries, key_block, preferred_element_type=jnp.float32) * 0.125
    )
    key_pos = block_start + jnp.arange(key_block.shape[0], dtype=jnp.int32)
    return jnp.where(key_pos[None, None, :] < length, scores, neg_big)


def keep_state(state):
    return state


def attention_forward(queries, keys_blocks, values_blocks, block_starts, length):
    num_rows, num_heads, head_dim = queries.shape

    def online_step(carried, scan_item):
        key_block, value_block, block_start = scan_item

        def online_live_block(state):
            run_max, run_sum, accum = state
            scores = block_scores(queries, key_block, block_start, length)
            new_max = jnp.maximum(run_max, jnp.max(scores, axis=-1))
            factor = jnp.exp(run_max - new_max)
            weights = jnp.exp(scores - new_max[..., None])
            run_sum = run_sum * factor + jnp.sum(weights, axis=-1)
            accum = accum * factor.T[..., None] + jnp.einsum(
                "hrk,khd->rhd",
                weights.astype(jnp.bfloat16),
                value_block,
                preferred_element_type=jnp.float32,
            )
            return (new_max, run_sum, accum)

        return (lax.cond(block_start < length, online_live_block, keep_state, carried), None)

    start_state = (
        jnp.full((num_heads, num_rows), neg_big, jnp.float32),
        jnp.zeros((num_heads, num_rows), jnp.float32),
        jnp.zeros((num_rows, num_heads, head_dim), jnp.float32),
    )
    run_max, run_sum, accum = lax.scan(
        online_step, start_state, (keys_blocks, values_blocks, block_starts)
    )[0]
    log_sum = run_max + jnp.log(run_sum)
    attended = accum / run_sum.T[..., None]
    return (log_sum, attended)


def attention_backward(
    queries, keys_blocks, values_blocks, block_starts, length, log_sum, d_heads, row_delta
):
    num_rows, num_heads, head_dim = queries.shape

    def grad_step(d_query, scan_item):
        key_block, value_block, block_start = scan_item

        def grad_live_block(state):
            probs = jnp.exp(
                block_scores(queries, key_block, block_start, length) - log_sum[..., None]
            )
            d_probs = jnp.einsum(
                "rhd,khd->hrk", d_heads, value_block, preferred_element_type=jnp.float32
            )
            d_value = jnp.einsum(
                "hrk,rhd->khd",
                probs.astype(jnp.bfloat16),
                d_heads,
                preferred_element_type=jnp.float32,
            )
            d_scores = (probs * (d_probs - row_delta[..., None])).astype(jnp.bfloat16)
            d_key = (
                jnp.einsum("hrk,rhd->khd", d_scores, queries, preferred_element_type=jnp.float32)
                * 0.125
            )
            return (
                state
                + jnp.einsum(
                    "hrk,khd->rhd", d_scores, key_block, preferred_element_type=jnp.float32
                ),
                (d_key, d_value),
            )

        def dead_block(state):
            return (
                state,
                (
                    jnp.zeros(key_block.shape, jnp.float32),
                    jnp.zeros(value_block.shape, jnp.float32),
                ),
            )

        return lax.cond(block_start < length, grad_live_block, dead_block, d_query)

    d_query, key_value = lax.scan(
        grad_step,
        jnp.zeros((num_rows, num_heads, head_dim), jnp.float32),
        (keys_blocks, values_blocks, block_starts),
    )
    return (d_query * 0.125, key_value[0], key_value[1])


def shards(
    hidden_in,
    input_proj,
    output_proj,
    up_proj,
    down_proj,
    bias_rows,
    up_bias,
    norm_gains,
    norm_shifts,
    cotangent,
    lengths,
):
    num_batches, num_rows, model_width = hidden_in.shape
    head_dim = model_width // HEADS
    row_pos = lax.axis_index("ctx") * num_rows + jnp.arange(num_rows, dtype=jnp.int32)
    seq_len = num_rows * lax.axis_size("ctx")
    block_len = min(512, seq_len)
    num_blocks = seq_len // block_len
    block_starts = jnp.arange(num_blocks, dtype=jnp.int32) * block_len
    outputs = []
    grad_inputs = []
    summed = None
    for batch in range(num_batches):
        gathered = (
            lax.all_gather(input_proj, ("dp", "ctx"), axis=1, tiled=True),
            lax.all_gather(output_proj, ("dp", "ctx"), axis=0, tiled=True),
            lax.all_gather(up_proj, ("dp", "ctx"), axis=0, tiled=True),
            lax.all_gather(down_proj, ("dp", "ctx"), axis=0, tiled=True),
            lax.all_gather(bias_rows, ("dp", "ctx"), axis=1, tiled=True),
            lax.all_gather(up_bias, ("dp", "ctx"), axis=0, tiled=True),
            lax.all_gather(norm_gains, ("dp", "ctx"), axis=1, tiled=True),
            lax.all_gather(norm_shifts, ("dp", "ctx"), axis=1, tiled=True),
        )
        weight_in, weight_out, weight_up, weight_down, bias_all, bias_upper, gain_all, shift_all = (
            gathered
        )
        bias_vals = bias_all.astype(jnp.float32)
        upper_bias = bias_upper.astype(jnp.float32)
        gain_vals = gain_all.astype(jnp.float32)
        shift_vals = shift_all.astype(jnp.float32)
        tokens = hidden_in[batch]
        length = lengths[batch]
        queries = (matmul(tokens, weight_in[0]) + bias_vals[0]).astype(jnp.bfloat16)
        keys_loc = matmul(tokens, weight_in[1]).astype(jnp.bfloat16)
        values_loc = (matmul(tokens, weight_in[2]) + bias_vals[1]).astype(jnp.bfloat16)
        keys_all, values_all = (
            lax.all_gather(keys_loc, "ctx", axis=0, tiled=True),
            lax.all_gather(values_loc, "ctx", axis=0, tiled=True),
        )
        query_heads = queries.reshape(num_rows, HEADS, head_dim)
        keys_blocks = keys_all.reshape(num_blocks, block_len, HEADS, head_dim)
        values_blocks = values_all.reshape(num_blocks, block_len, HEADS, head_dim)
        log_sum, attended = attention_forward(
            query_heads, keys_blocks, values_blocks, block_starts, length
        )
        heads_out = attended.reshape(num_rows, model_width).astype(jnp.bfloat16)
        first_sum = tokens.astype(jnp.float32) + matmul(heads_out, weight_out) + bias_vals[2]
        normed, first_back = jax.vjp(layer_norm, first_sum, gain_vals[0], shift_vals[0])
        normed_low = normed.astype(jnp.bfloat16)
        upper = matmul(normed_low, weight_up) + upper_bias
        activ_full, gelu_back = jax.vjp(gelu_exact, upper)
        activated = activ_full.astype(jnp.bfloat16)
        second_sum = normed + matmul(activated, weight_down) + bias_vals[3]
        layer_out, second_back = jax.vjp(layer_norm, second_sum, gain_vals[1], shift_vals[1])
        outputs.append(layer_out.astype(jnp.bfloat16))
        gathered = (
            lax.all_gather(input_proj, ("dp", "ctx"), axis=1, tiled=True),
            lax.all_gather(output_proj, ("dp", "ctx"), axis=0, tiled=True),
            lax.all_gather(up_proj, ("dp", "ctx"), axis=0, tiled=True),
            lax.all_gather(down_proj, ("dp", "ctx"), axis=0, tiled=True),
            lax.all_gather(bias_rows, ("dp", "ctx"), axis=1, tiled=True),
            lax.all_gather(up_bias, ("dp", "ctx"), axis=0, tiled=True),
            lax.all_gather(norm_gains, ("dp", "ctx"), axis=1, tiled=True),
            lax.all_gather(norm_shifts, ("dp", "ctx"), axis=1, tiled=True),
        )
        weight_in, weight_out, weight_up, weight_down = (
            gathered[0],
            gathered[1],
            gathered[2],
            gathered[3],
        )
        row_live = (row_pos < length).astype(jnp.float32)[:, None]
        d_second, gain_two, shift_two = second_back(cotangent[batch].astype(jnp.float32) * row_live)
        d_ffn = d_second.astype(jnp.bfloat16)
        grad_down = matmul_tn(activated, d_ffn)
        d_upper = gelu_back(matmul_nt(d_ffn, weight_down))[0].astype(jnp.bfloat16)
        grad_upper = matmul_tn(normed_low, d_upper)
        d_normed = d_second + matmul_nt(d_upper, weight_up)
        d_first, gain_one, shift_one = first_back(d_normed)
        d_branch = d_first.astype(jnp.bfloat16)
        grad_outproj = matmul_tn(heads_out, d_branch)
        d_heads = (
            matmul_nt(d_branch, weight_out).astype(jnp.bfloat16).reshape(num_rows, HEADS, head_dim)
        )
        row_delta = jnp.sum(d_heads.astype(jnp.float32) * attended, axis=-1).T
        d_query, d_keys, d_values = attention_backward(
            query_heads,
            keys_blocks,
            values_blocks,
            block_starts,
            length,
            log_sum,
            d_heads,
            row_delta,
        )
        keys_sum, values_sum = (
            lax.psum_scatter(
                d_keys.reshape(seq_len, model_width).astype(jnp.bfloat16),
                "ctx",
                scatter_dimension=0,
                tiled=True,
            ).astype(jnp.float32),
            lax.psum_scatter(
                d_values.reshape(seq_len, model_width).astype(jnp.bfloat16),
                "ctx",
                scatter_dimension=0,
                tiled=True,
            ).astype(jnp.float32),
        )
        d_query_low = d_query.reshape(num_rows, model_width).astype(jnp.bfloat16)
        d_keys_low = keys_sum.astype(jnp.bfloat16)
        d_values_low = values_sum.astype(jnp.bfloat16)
        grad_inputs.append(
            d_first
            + matmul_nt(d_query_low, weight_in[0])
            + matmul_nt(d_keys_low, weight_in[1])
            + matmul_nt(d_values_low, weight_in[2])
        )
        grad_inproj = jnp.stack(
            [
                matmul_tn(tokens, d_query_low),
                matmul_tn(tokens, d_keys_low),
                matmul_tn(tokens, d_values_low),
            ]
        )
        grad_biases = jnp.stack(
            [
                column_sum(d_query_low),
                column_sum(d_values_low),
                column_sum(d_branch),
                column_sum(d_ffn),
            ]
        )
        grad_upbias = column_sum(d_upper)
        grad_gainrows = jnp.stack([gain_one, gain_two])
        grad_shiftrows = jnp.stack([shift_one, shift_two])
        local_grads = (
            lax.psum_scatter(grad_inproj, ("dp", "ctx"), scatter_dimension=1, tiled=True),
            lax.psum_scatter(grad_outproj, ("dp", "ctx"), scatter_dimension=0, tiled=True),
            lax.psum_scatter(grad_upper, ("dp", "ctx"), scatter_dimension=0, tiled=True),
            lax.psum_scatter(grad_down, ("dp", "ctx"), scatter_dimension=0, tiled=True),
            lax.psum_scatter(grad_biases, ("dp", "ctx"), scatter_dimension=1, tiled=True),
            lax.psum_scatter(grad_upbias, ("dp", "ctx"), scatter_dimension=0, tiled=True),
            lax.psum_scatter(grad_gainrows, ("dp", "ctx"), scatter_dimension=1, tiled=True),
            lax.psum_scatter(grad_shiftrows, ("dp", "ctx"), scatter_dimension=1, tiled=True),
        )
        if batch == 0:
            summed = tuple(local_grads)
        else:
            summed = tuple((earlier + addend for earlier, addend in zip(summed, local_grads)))
    return (
        jnp.stack(outputs),
        jnp.stack(grad_inputs),
        summed[0],
        summed[1],
        summed[2],
        summed[3],
        summed[4],
        summed[5],
        summed[6],
        summed[7],
    )


def general(mesh):
    in_specs = (
        P("dp", "ctx", None),
        P(None, ("dp", "ctx"), None),
        P(("dp", "ctx"), None),
        P(("dp", "ctx"), None),
        P(("dp", "ctx"), None),
        P(None, ("dp", "ctx")),
        P(("dp", "ctx")),
        P(None, ("dp", "ctx")),
        P(None, ("dp", "ctx")),
        P("dp", "ctx", None),
        P("dp"),
    )
    out_specs = (
        P("dp", "ctx", None),
        P("dp", "ctx", None),
        P(None, ("dp", "ctx"), None),
        P(("dp", "ctx"), None),
        P(("dp", "ctx"), None),
        P(("dp", "ctx"), None),
        P(None, ("dp", "ctx")),
        P(("dp", "ctx")),
        P(None, ("dp", "ctx")),
        P(None, ("dp", "ctx")),
    )
    return jax.shard_map(shards, mesh=mesh, in_specs=in_specs, out_specs=out_specs, check_vma=False)


ID = pl.DeviceIdType.MESH


class Grid(NamedTuple):
    nx: int
    nmaj: int
    nmin: int


class Spot(NamedTuple):
    x: object
    core: object
    maj: object
    min: object


def here(grid):
    dp = lax.axis_index("dp")
    ctx = lax.axis_index("ctx")
    return Spot(dp // 2, dp % 2, ctx // grid.nmin, ctx % grid.nmin)


def device(grid, spot):
    return (2 * spot.x + spot.core, spot.maj * grid.nmin + spot.min)


def chunk_of(grid, x, core, maj, mnr):
    return ((2 * x + core) * grid.nmaj + maj) * grid.nmin + mnr


def near_first(pos, size, step):
    if size == 4:
        half = pos // 2
        return [pos, pos + 1 - 2 * (pos % 2), 2 - half, 3 - 3 * half][step]
    return (pos + step) % size


def chip_steps(grid):
    steps = itertools.product(range(grid.nmaj), range(grid.nx), range(grid.nmin))
    return sorted(steps, key=lambda s: (s[1] + s[2], s))


def chip_at(grid, me, step):
    return (
        near_first(me.x, grid.nx, step[1]),
        near_first(me.maj, grid.nmaj, step[0]),
        near_first(me.min, grid.nmin, step[2]),
    )


def tree_lines(grid, me, chip, x_first):
    sx, smaj, smin = chip
    on_line = (sx == me.x) & (smin == me.min)
    same_x, same_min = sx == me.x, smin == me.min
    every = smin == smin
    return (
        ("maj", me.maj, smaj, grid.nmaj, on_line),
        ("x", me.x, sx, grid.nx, same_min if x_first else every),
        ("min", me.min, smin, grid.nmin, every if x_first else same_x),
    )


def down_hops(grid, me, chip, x_first):
    hops = []
    for field, pos, start, size, online in tree_lines(grid, me, chip, x_first):
        if size == 2:
            hops.append((online & (pos == start), me._replace(**{field: 1 - pos})))
        elif size > 2:
            hops.append((online & (pos >= start) & (pos < size - 1), me._replace(**{field: pos + 1})))
            hops.append((online & (pos <= start) & (pos > 0), me._replace(**{field: pos - 1})))
    return hops


def up_hops(grid, me, chip, x_first):
    hops, slot = [], 0
    for field, pos, start, size, online in tree_lines(grid, me, chip, x_first):
        if size == 2:
            hops.append((online & (pos != start), me._replace(**{field: 1 - pos}), slot))
            slot += 1
        elif size > 2:
            hops.append((online & (pos > start), me._replace(**{field: pos - 1}), slot))
            hops.append((online & (pos < start), me._replace(**{field: pos + 1}), slot + 1))
            slot += 2
    return hops


def num_dirs(grid):
    return sum(1 if size == 2 else 2 for size in grid if size > 1)


def remote(grid, src, dst, send_sem, recv_sem, target):
    return pltpu.make_async_remote_copy(
        src_ref=src, dst_ref=dst, send_sem=send_sem, recv_sem=recv_sem,
        device_id=device(grid, target), device_id_type=ID,
    )


def arrived(ref, sem):
    pltpu.make_async_copy(ref, ref, sem).wait()


def greet(grid, me):
    barrier = pltpu.get_barrier_semaphore()
    others = []
    for step in range(grid.nmaj):
        for flip in range(2):
            if step or flip:
                others.append(me._replace(maj=(me.maj + step) % grid.nmaj, core=(me.core + flip) % 2))
    others.append(me._replace(x=1 - me.x))
    others.append(me._replace(min=1 - me.min))
    for other in others:
        pl.semaphore_signal(barrier, inc=1, device_id=device(grid, other), device_id_type=ID)
    pl.semaphore_wait(barrier, len(others))


def gather_kernel(grid, pieces, pack_ref, hid_ref, cot_ref, g_pack, h_full, cot_own,
                  local_sem, w_recv, w_send, w_part, h_recv, h_out, h_min, h_part, c_recv, c_send):
    me = here(grid)
    partner = me._replace(core=1 - me.core)
    greet(grid, me)
    pos = me.maj * grid.nmin + me.min
    carrier = me.core == me.maj // 2

    own_pack = pltpu.make_async_copy(pack_ref, g_pack.at[chunk_of(grid, me.x, me.core, me.maj, me.min)], local_sem)
    own_pack.start()

    def hidden_out(k, go):
        dest = me._replace(maj=2 * me.core + k)

        @pl.when(dest.maj != me.maj)
        def _():
            copy = remote(grid, hid_ref.at[k], h_full.at[pos], h_out.at[k], h_recv.at[pos], dest)
            copy.start() if go else copy.wait_send()

        if go:
            @pl.when(dest.maj == me.maj)
            def _():
                pltpu.make_async_copy(hid_ref.at[k], h_full.at[pos], h_recv.at[pos]).start()

    def cotangent_out(k, go):
        dest = me._replace(maj=2 * me.core + k, core=me.maj // 2)
        stays = (dest.maj == me.maj) & carrier
        slot = me.maj % 2

        @pl.when(jnp.logical_not(stays))
        def _():
            copy = remote(grid, cot_ref.at[k], cot_own.at[slot], c_send.at[k], c_recv.at[slot], dest)
            copy.start() if go else copy.wait_send()

        if go:
            @pl.when(stays)
            def _():
                pltpu.make_async_copy(cot_ref.at[k], cot_own.at[slot], c_recv.at[slot]).start()

    def weight_step(part, step, go):
        chip = chip_at(grid, me, step)
        sx, smaj, smin = chip
        own = sum(step) == 0
        chunk = chunk_of(grid, sx, me.core, smaj, smin)
        index = (sx * grid.nmaj + smaj) * grid.nmin + smin
        rows = pl.ds(*pieces[part])
        dst = g_pack.at[chunk, rows]
        src = pack_ref.at[rows] if own else dst
        recv = w_recv.at[part, chunk]
        if go and not own:
            arrived(dst, recv)
        for d, (cond, target) in enumerate(down_hops(grid, me, chip, part % 2 == 0)):
            @pl.when(cond)
            def _(d=d, target=target):
                copy = remote(grid, src, dst, w_send.at[part, index, d], recv, target)
                copy.start() if go else copy.wait_send()
        copy = remote(grid, src, dst, w_part.at[part, index], recv, partner)
        copy.start() if go else copy.wait_send()

    def hidden_step(jmaj, jmin, go):
        bmin = near_first(me.min, grid.nmin, jmin)
        p = near_first(me.maj, grid.nmaj, jmaj) * grid.nmin + bmin
        block = h_full.at[p]
        if go:
            arrived(block, h_recv.at[p])
        if jmin == 0:
            copy = remote(grid, block, block, h_min.at[p], h_recv.at[p], me._replace(min=1 - me.min))
            copy.start() if go else copy.wait_send()
        copy = remote(grid, block, block, h_part.at[p], h_recv.at[p], partner)
        copy.start() if go else copy.wait_send()

    blocks = [(jmaj, jmin) for jmin in range(grid.nmin) for jmaj in range(grid.nmaj)]
    order = [(part, step) for step in chip_steps(grid) for part in range(len(pieces))]

    for go in (True, False):
        for k in range(2):
            hidden_out(k, go)
        for part in range(len(pieces)):
            weight_step(part, (0, 0, 0), go)
        for k in range(2):
            cotangent_out(k, go)

        @pl.when(carrier)
        def _(go=go):
            for jmaj, jmin in blocks:
                hidden_step(jmaj, jmin, go)

        for part, step in order:
            if sum(step):
                weight_step(part, step, go)
        if go:
            for part, step in order:
                chunk = chunk_of(grid, step[1], 1 - me.core, step[0], step[2])
                arrived(g_pack.at[chunk, pl.ds(*pieces[part])], w_recv.at[part, chunk])

            @pl.when(jnp.logical_not(carrier))
            def _():
                for p in range(grid.nmaj * grid.nmin):
                    arrived(h_full.at[p], h_recv.at[p])

            for k in range(2):
                arrived(cot_own.at[k], c_recv.at[k])
    own_pack.wait()


def gather_all(grid, pieces, pack, hid, cot):
    chips = grid.nx * grid.nmaj * grid.nmin
    npos = grid.nmaj * grid.nmin
    nd = num_dirs(grid)
    np_ = len(pieces)
    sems = pltpu.SemaphoreType.DMA
    rows, width = hid.shape[1:]
    return pl.pallas_call(
        functools.partial(gather_kernel, grid, pieces),
        out_shape=(
            jax.ShapeDtypeStruct((2 * chips,) + pack.shape, pack.dtype),
            jax.ShapeDtypeStruct((npos, rows, width), hid.dtype),
            jax.ShapeDtypeStruct((2, rows, width), cot.dtype),
        ),
        in_specs=[pl.BlockSpec(memory_space=pltpu.VMEM)] * 3,
        out_specs=[pl.BlockSpec(memory_space=pl.ANY)] * 3,
        scratch_shapes=[
            sems, sems((np_, 2 * chips)), sems((np_, chips, nd)), sems((np_, chips)),
            sems((npos,)), sems((2,)), sems((npos,)), sems((npos,)), sems((2,)), sems((2,)),
        ],
        compiler_params=pltpu.CompilerParams(collective_id=0, has_side_effects=True),
        name="gather_all",
    )(pack, hid, cot)


def reduce_kernel(grid, pieces, g_pack, gi_part, gi_own, lo_own, sum_pack, grad_in, layer_out,
                  mine, theirs, below, total, gi_mine, gi_theirs, gi_below, gi_final,
                  m_sem, t_send, t_recv, b_recv, b_send, i_load, i_tsend, i_trecv, i_msend, i_mrecv,
                  i_fsend, i_frecv, l_send, l_recv):
    me = here(grid)
    partner = me._replace(core=1 - me.core)
    greet(grid, me)
    order = [(part, step) for step in chip_steps(grid) for part in range(len(pieces))][::-1]

    def layer_out_back(j, go):
        dest = me._replace(maj=2 * me.core + j, core=me.maj // 2)
        stays = (dest.maj == me.maj) & (dest.core == me.core)
        slot = me.maj % 2

        @pl.when(jnp.logical_not(stays))
        def _():
            copy = remote(grid, lo_own.at[j], layer_out.at[slot], l_send.at[j], l_recv.at[slot], dest)
            copy.start() if go else copy.wait_send()

        if go:
            @pl.when(stays)
            def _():
                pltpu.make_async_copy(lo_own.at[j], layer_out.at[slot], l_recv.at[slot]).start()

    def load(step, go):
        sx, smaj, smin = chip_at(grid, me, step)
        index = (sx * grid.nmaj + smaj) * grid.nmin + smin
        other = g_pack.at[chunk_of(grid, sx, 1 - me.core, smaj, smin)]
        copy = remote(grid, other, theirs.at[index], t_send.at[index], t_recv.at[index], partner)
        if go:
            pltpu.make_async_copy(g_pack.at[chunk_of(grid, sx, me.core, smaj, smin)], mine.at[index], m_sem.at[index]).start()
            copy.start()
        else:
            copy.wait_send()

    def weight_step(part, step, go):
        chip = chip_at(grid, me, step)
        sx, smaj, smin = chip
        own = sum(step) == 0
        index = (sx * grid.nmaj + smaj) * grid.nmin + smin
        lo, size = pieces[part]
        rows = pl.ds(lo, size)
        x_first = part % 2 == 0
        if go:
            if part == len(pieces) - 1:
                arrived(mine.at[index], m_sem.at[index])
                arrived(theirs.at[index], t_recv.at[index])
            total[pl.ds(0, size)] = mine[index, rows].astype(jnp.float32) + theirs[index, rows].astype(jnp.float32)
            for d, (cond, _) in enumerate(down_hops(grid, me, chip, x_first)):
                @pl.when(cond)
                def _(d=d):
                    arrived(below.at[d, index, rows], b_recv.at[d, part, index])
                    total[pl.ds(0, size)] += below[d, index, rows].astype(jnp.float32)
            if own:
                sum_pack[rows] = total[pl.ds(0, size)]
            else:
                mine[index, rows] = total[pl.ds(0, size)].astype(jnp.bfloat16)
        if not own:
            for cond, target, d in up_hops(grid, me, chip, x_first):
                @pl.when(cond)
                def _(d=d, target=target):
                    copy = remote(grid, mine.at[index, rows], below.at[d, index, rows], b_send.at[part, index],
                                  b_recv.at[d, part, index], target)
                    copy.start() if go else copy.wait_send()

    half = grid.nmaj // 2

    def swap_in(go):
        for j in range(half):
            for jmin in range(grid.nmin):
                away = (half * partner.core + j) * grid.nmin + jmin
                home = (half * me.core + j) * grid.nmin + jmin
                at = j * grid.nmin + jmin
                copy = remote(grid, gi_part.at[away], gi_theirs.at[at], i_tsend.at[at], i_trecv.at[at], partner)
                if go:
                    pltpu.make_async_copy(gi_part.at[home], gi_mine.at[at], i_load.at[at]).start()
                    copy.start()
                else:
                    copy.wait_send()

    def across(j, go):
        other = 1 - me.min
        at = j * grid.nmin + other
        if go:
            arrived(gi_mine.at[at], i_load.at[at])
            arrived(gi_theirs.at[at], i_trecv.at[at])
            gi_mine[at] = (gi_mine[at].astype(jnp.float32) + gi_theirs[at].astype(jnp.float32)).astype(jnp.bfloat16)
        copy = remote(grid, gi_mine.at[at], gi_below.at[j], i_msend.at[j], i_mrecv.at[j], me._replace(min=other))
        copy.start() if go else copy.wait_send()

    def home(j, go):
        at = j * grid.nmin + me.min
        if go:
            arrived(gi_mine.at[at], i_load.at[at])
            arrived(gi_theirs.at[at], i_trecv.at[at])
            arrived(gi_below.at[j], i_mrecv.at[j])
            gi_final[j] = (
                gi_own[j] + gi_mine[at].astype(jnp.float32) + gi_theirs[at].astype(jnp.float32)
                + gi_below[j].astype(jnp.float32)
            )
        dest = me._replace(maj=2 * me.core + j, core=me.maj // 2)
        stays = (dest.maj == me.maj) & (dest.core == me.core)
        slot = me.maj % 2

        @pl.when(jnp.logical_not(stays))
        def _():
            copy = remote(grid, gi_final.at[j], grad_in.at[slot], i_fsend.at[j], i_frecv.at[slot], dest)
            copy.start() if go else copy.wait_send()

        if go:
            @pl.when(stays)
            def _():
                pltpu.make_async_copy(gi_final.at[j], grad_in.at[slot], i_frecv.at[slot]).start()

    steps = [step for part, step in order if part == 0]
    for go in (True, False):
        for step in steps[:2]:
            load(step, go)
        swap_in(go)
        for step in steps[2:]:
            load(step, go)
        for j in range(half):
            layer_out_back(j, go)
        for n, (part, step) in enumerate(order):
            weight_step(part, step, go)
            if n == 7:
                for j in range(half):
                    across(j, go)
            if n == 15:
                for j in range(half):
                    home(j, go)
    for k in range(2):
        arrived(layer_out.at[k], l_recv.at[k])
        arrived(grad_in.at[k], i_frecv.at[k])


def reduce_all(grid, pieces, g_pack, gi_part, gi_own, lo_own):
    chips = grid.nx * grid.nmaj * grid.nmin
    nd = num_dirs(grid)
    np_ = len(pieces)
    half = grid.nmaj // 2
    sems = pltpu.SemaphoreType.DMA
    vmem, anyw = pl.BlockSpec(memory_space=pltpu.VMEM), pl.BlockSpec(memory_space=pl.ANY)
    rows, width = gi_part.shape[1:]
    pack_rows = g_pack.shape[1]
    low = jnp.bfloat16
    return pl.pallas_call(
        functools.partial(reduce_kernel, grid, pieces),
        out_shape=(
            jax.ShapeDtypeStruct((pack_rows, width), jnp.float32),
            jax.ShapeDtypeStruct((2, rows, width), jnp.float32),
            jax.ShapeDtypeStruct((2, rows, width), low),
        ),
        in_specs=[anyw, anyw, vmem, vmem],
        out_specs=[vmem, anyw, anyw],
        scratch_shapes=[
            pltpu.VMEM((chips, pack_rows, width), low),
            pltpu.VMEM((chips, pack_rows, width), low),
            pltpu.VMEM((nd, chips, pack_rows, width), low),
            pltpu.VMEM((max(n for _, n in pieces), width), jnp.float32),
            pltpu.VMEM((half * grid.nmin, rows, width), low),
            pltpu.VMEM((half * grid.nmin, rows, width), low),
            pltpu.VMEM((half, rows, width), low),
            pltpu.VMEM((half, rows, width), jnp.float32),
            sems((chips,)), sems((chips,)), sems((chips,)), sems((nd, np_, chips)), sems((np_, chips)),
            sems((half * grid.nmin,)), sems((half * grid.nmin,)), sems((half * grid.nmin,)),
            sems((half,)), sems((half,)), sems((half,)), sems((2,)), sems((half,)), sems((2,)),
        ],
        compiler_params=pltpu.CompilerParams(collective_id=1, has_side_effects=True, vmem_limit_bytes=64000 * 1024),
        name="reduce_all",
    )(g_pack, gi_part, gi_own, lo_own)


def split_rows(model_width, hidden_width, count):
    shard = model_width // count
    return shard, hidden_width // count


def pack_small(count, bias_rows, up_bias, norm_gains, norm_shifts):
    def cut(rows):
        return rows.reshape(rows.shape[0], count, -1).transpose(1, 0, 2).reshape(count, -1)

    return jnp.concatenate([cut(bias_rows), cut(up_bias[None]), cut(norm_gains), cut(norm_shifts)], axis=1)


def unpack_small(flat, width, ff):
    count = flat.shape[0]
    shard, ffs = width // count, ff // count

    def join(lo, rows, size):
        return flat[:, lo : lo + rows * size].reshape(count, rows, size).transpose(1, 0, 2).reshape(rows, count * size)

    at = 0
    out = []
    for rows, size in ((4, shard), (1, ffs), (2, shard), (2, shard)):
        out.append(join(at, rows, size))
        at += rows * size
    return out[0], out[1][0], out[2], out[3]


def local_layer(weights, small, hidden, own, cot, length, own_pos):
    weight_in, weight_out, weight_up, weight_down = weights
    bias_vals, upper_bias, gain_vals, shift_vals = [v.astype(jnp.float32) for v in small]
    num_rows, model_width = own.shape
    seq_len = hidden.shape[0]
    head_dim = model_width // HEADS
    queries = (matmul(own, weight_in[0]) + bias_vals[0]).astype(jnp.bfloat16)
    keys = matmul(hidden, weight_in[1]).astype(jnp.bfloat16)
    values = (matmul(hidden, weight_in[2]) + bias_vals[1]).astype(jnp.bfloat16)
    query_heads = queries.reshape(num_rows, HEADS, head_dim)
    keys_blocks = keys.reshape(1, seq_len, HEADS, head_dim)
    values_blocks = values.reshape(1, seq_len, HEADS, head_dim)
    block_starts = jnp.zeros((1,), jnp.int32)
    log_sum, attended = attention_forward(query_heads, keys_blocks, values_blocks, block_starts, length)
    heads_out = attended.reshape(num_rows, model_width).astype(jnp.bfloat16)
    first_sum = own.astype(jnp.float32) + matmul(heads_out, weight_out) + bias_vals[2]
    normed, first_back = jax.vjp(layer_norm, first_sum, gain_vals[0], shift_vals[0])
    normed_low = normed.astype(jnp.bfloat16)
    upper = matmul(normed_low, weight_up) + upper_bias
    activ_full, gelu_back = jax.vjp(gelu_exact, upper)
    activated = activ_full.astype(jnp.bfloat16)
    second_sum = normed + matmul(activated, weight_down) + bias_vals[3]
    layer_out, second_back = jax.vjp(layer_norm, second_sum, gain_vals[1], shift_vals[1])
    row_live = (own_pos < length).astype(jnp.float32)[:, None]
    d_second, gain_two, shift_two = second_back(cot.astype(jnp.float32) * row_live)
    d_ffn = d_second.astype(jnp.bfloat16)
    grad_down = matmul_tn(activated, d_ffn)
    d_upper = gelu_back(matmul_nt(d_ffn, weight_down))[0].astype(jnp.bfloat16)
    grad_upper = matmul_tn(normed_low, d_upper)
    d_normed = d_second + matmul_nt(d_upper, weight_up)
    d_first, gain_one, shift_one = first_back(d_normed)
    d_branch = d_first.astype(jnp.bfloat16)
    grad_outproj = matmul_tn(heads_out, d_branch)
    d_heads = matmul_nt(d_branch, weight_out).astype(jnp.bfloat16).reshape(num_rows, HEADS, head_dim)
    row_delta = jnp.sum(d_heads.astype(jnp.float32) * attended, axis=-1).T
    d_query, d_keys, d_values = attention_backward(
        query_heads, keys_blocks, values_blocks, block_starts, length, log_sum, d_heads, row_delta
    )
    d_query_low = d_query.reshape(num_rows, model_width).astype(jnp.bfloat16)
    d_keys_low = d_keys.reshape(seq_len, model_width).astype(jnp.bfloat16)
    d_values_low = d_values.reshape(seq_len, model_width).astype(jnp.bfloat16)
    grad_all = matmul_nt(d_keys_low, weight_in[1]) + matmul_nt(d_values_low, weight_in[2])
    grad_own = d_first + matmul_nt(d_query_low, weight_in[0])
    grad_in = jnp.stack([matmul_tn(own, d_query_low), matmul_tn(hidden, d_keys_low), matmul_tn(hidden, d_values_low)])
    grad_biases = jnp.stack(
        [column_sum(d_query_low), column_sum(d_values_low), column_sum(d_branch), column_sum(d_ffn)]
    )
    small_grads = (grad_biases, column_sum(d_upper), jnp.stack([gain_one, gain_two]), jnp.stack([shift_one, shift_two]))
    return (
        layer_out.astype(jnp.bfloat16), grad_all.astype(jnp.bfloat16), grad_own,
        (grad_in, grad_outproj, grad_upper, grad_down), small_grads,
    )


def pack_rows(count, w_in, w_out, w_up, w_down, small):
    width = w_out.shape[-1]
    shard = w_out.shape[0] // count
    cols = w_up.shape[-1] // width
    low = jnp.bfloat16
    rows = small.shape[1]
    return jnp.concatenate(
        [
            w_in.astype(low).reshape(3, count, shard, width).transpose(1, 0, 2, 3).reshape(count, 3 * shard, width),
            w_out.astype(low).reshape(count, shard, width),
            w_up.astype(low).reshape(count, shard, cols, width).transpose(0, 2, 1, 3).reshape(count, cols * shard, width),
            w_down.astype(low).reshape(count, -1, width),
            jnp.pad(small.astype(low)[:, None, :], ((0, 0), (0, 7), (0, width - rows))),
        ],
        axis=1,
    )


def fast_shards(
    grid, hidden_in, input_proj, output_proj, up_proj, down_proj, bias_rows, up_bias, norm_gains, norm_shifts,
    cotangent, lengths,
):
    count = 2 * grid.nx * grid.nmaj * grid.nmin
    width = hidden_in.shape[2]
    rows = hidden_in.shape[1]
    shard = output_proj.shape[0]
    ff = up_proj.shape[1]
    cols = ff // width
    ffs = down_proj.shape[0]
    low = jnp.bfloat16
    small_own = pack_small(1, bias_rows, up_bias, norm_gains, norm_shifts)
    counts = jnp.concatenate([lengths // 256, lengths % 256]).astype(low)[None]
    pack = pack_rows(1, input_proj, output_proj, up_proj, down_proj, jnp.concatenate([small_own, counts], axis=1))[0]
    num_small = small_own.shape[1]
    total_rows = pack.shape[0]
    cut = total_rows // 16 * 8
    pieces = ((0, cut), (cut, total_rows - cut))
    g_pack, h_full, cot_own = gather_all(grid, pieces, pack, hidden_in, cotangent)

    me = here(grid)
    a, b, c, d = 3 * shard, 4 * shard, (4 + cols) * shard, (4 + cols) * shard + ffs
    weights = (
        g_pack[:, :a].reshape(count, 3, shard, width).transpose(1, 0, 2, 3).reshape(3, width, width),
        g_pack[:, a:b].reshape(width, width),
        g_pack[:, b:c].reshape(count, cols, shard, width).transpose(0, 2, 1, 3).reshape(width, ff),
        g_pack[:, c:d].reshape(ff, width),
    )
    flat = g_pack[:, d]
    small = unpack_small(flat[:, :num_small], width, ff)
    keeper = (2 * me.x + me.maj // 2) * (grid.nmaj * grid.nmin)
    digits = lax.dynamic_slice(flat, (keeper, num_small), (1, 4))[0].astype(jnp.int32)
    length = jnp.where(me.maj % 2 == 0, digits[0] * 256 + digits[2], digits[1] * 256 + digits[3])
    half = grid.nmaj // 2
    own_blocks = [(half * me.core + j) * grid.nmin + me.min for j in range(half)]
    own = jnp.concatenate([lax.dynamic_index_in_dim(h_full, p, 0, keepdims=False) for p in own_blocks])
    own_pos = jnp.concatenate([p * rows + jnp.arange(rows, dtype=jnp.int32) for p in own_blocks])
    layer_out, grad_all, grad_own, grads, small_grads = local_layer(
        weights, small, h_full.reshape(-1, width), own, cot_own.reshape(-1, width), length, own_pos
    )
    g_sums = pack_rows(count, *grads, pack_small(count, *small_grads))
    sum_pack, grad_input, layer_out = reduce_all(
        grid, pieces, g_sums, grad_all.reshape(-1, rows, width), grad_own.reshape(half, rows, width),
        layer_out.reshape(half, rows, width),
    )
    g_small = unpack_small(sum_pack[d : d + 1, :num_small], shard, ffs)
    return (
        layer_out,
        grad_input,
        sum_pack[:a].reshape(3, shard, width),
        sum_pack[a:b],
        sum_pack[b:c].reshape(cols, shard, width).transpose(1, 0, 2).reshape(shard, ff),
        sum_pack[c:d],
        g_small[0],
        g_small[1],
        g_small[2],
        g_small[3],
    )


def solution(mesh):
    sizes = (mesh.shape["dp"], mesh.shape["ctx"])
    if sizes != (4, 8):
        return general(mesh)
    grid = Grid(sizes[0] // 2, 4, sizes[1] // 4)
    axes = ("dp", "ctx")
    in_specs = (
        P("dp", "ctx", None), P(None, axes, None), P(axes, None), P(axes, None), P(axes, None), P(None, axes),
        P(axes), P(None, axes), P(None, axes), P("dp", "ctx", None), P("dp"),
    )
    out_specs = (
        P("dp", "ctx", None), P("dp", "ctx", None), P(None, axes, None), P(axes, None), P(axes, None), P(axes, None),
        P(None, axes), P(axes), P(None, axes), P(None, axes),
    )
    return jax.shard_map(
        functools.partial(fast_shards, grid), mesh=mesh, in_specs=in_specs, out_specs=out_specs, check_vma=False
    )
```
